256 devices in a mesh: samp: 8 (over z), snp: 32 (over x, y, core).
Axes of the slice: x: 4, y: 4, z: 8, core: 2. Of those that a mesh axis runs over, the one named last changes fastest.
Arguments:
- genotypes: bfloat16 [16384, 65536], P('samp', 'snp'), may hold values from 0 to 3, as said below
- frequency: float32 [65536], P('snp'), may hold values from 0.03 to 0.97
- seed_matrix: float32 [32, 65536], P(None, 'snp'), may hold values from -6 to 6
Outputs:
- sample_basis: bfloat16 [32, 16384], P(None, 'samp')
- snp_basis: bfloat16 [32, 65536], P(None, 'snp')
The draws below stay inside these ranges and needn't reach their ends.
Inputs may be any that keep to these rules, and one draw needn't show every extreme that they name: `genotypes`: dosages 0, 1, 2; the value 3 marks a missing call.
All inputs are finite; a program needn't handle non-finite values.
Results may differ from the reference program's by a relative error of at most 0.025.
Values may be sent and summed in bfloat16 or wider, within the bound.
A program may use at most 64 MiB of HBM per device.

```python
import jax
import jax.numpy as jnp
from jax import lax

K = 32
S_DEV = 2048
M_DEV = 2048
ITERS = 6
SAMPLES = 16384
SNPS = 65536


population_count = 4


def ancestral_codes(key):
    base = jax.random.randint(jax.random.fold_in(key, 5), (1, SNPS), 8, 57)
    offsets = jax.random.randint(jax.random.fold_in(key, 7), (population_count, SNPS), -6, 7)
    return jnp.clip(base + offsets, 2, 62).astype(jnp.int32)


def draw_frequency(key, part):
    codes = ancestral_codes(key)
    return (jnp.sum(codes, axis=0).astype(jnp.float32) / jnp.float32(64 * population_count)).astype(jnp.float32)


def draw_genotypes(key, part):
    codes = ancestral_codes(key)
    blocks = SAMPLES // S_DEV

    def one_block(index):
        sub = jax.random.fold_in(jax.random.fold_in(key, 101), index)
        key_weight, key_main, key_first, key_second, key_miss = jax.random.split(sub, 5)
        labels = jax.random.randint(key_main, (S_DEV, 1), 0, population_count)
        dominant = (labels == jnp.arange(population_count, dtype=jnp.int32)[None, :]).astype(jnp.int32)
        weights = jax.random.randint(key_weight, (S_DEV, population_count), 0, 5) + 12 * dominant
        total = jnp.sum(weights, axis=1, keepdims=True) * 64
        numer = jnp.dot(weights, codes)
        first = jax.random.randint(key_first, (S_DEV, SNPS), 0, total)
        second = jax.random.randint(key_second, (S_DEV, SNPS), 0, total)
        dosage = (first < numer).astype(jnp.int32) + (second < numer).astype(jnp.int32)
        missing = jax.random.randint(key_miss, (S_DEV, SNPS), 0, 32) == 0
        return jnp.where(missing, 3, dosage).astype(jnp.float32).astype(jnp.bfloat16)
    pieces = lax.map(one_block, jnp.arange(blocks, dtype=jnp.int32))
    return pieces.reshape(SAMPLES, SNPS)


def block_levels(own_key, dims, cuts, smallest, largest):
    factor_of = 1.0
    for position, parts in cuts:
        steps = jax.random.uniform(jax.random.fold_in(jax.random.fold_in(own_key, 6), position), (parts,), jnp.float32, smallest / len(cuts), largest / len(cuts))
        factor_of = factor_of * jnp.repeat(jnp.exp(steps), dims[position] // parts).reshape((-1,) + (1,) * (len(dims) - 1 - position))
    return factor_of


def normal_values(own_key, shape, scale, most, cuts=(), held_as=jnp.bfloat16):
    drawn = jax.random.normal(own_key, shape, jnp.float32) * scale
    if len(cuts) > 0:
        drawn = block_levels(own_key, shape, cuts, -0.22, 0.18) * drawn
    return jnp.clip(drawn, min=-most, max=most).astype(held_as)


def setup_inputs(seed: int = 0) -> dict:
    seeds = jax.random.split(jax.random.key(seed), 4)
    return {
        "genotypes": draw_genotypes(jax.random.fold_in(seeds[3], 71), 0),
        "frequency": draw_frequency(jax.random.fold_in(seeds[3], 71), 0),
        "seed_matrix": normal_values(seeds[2], (K, SNPS), 1.0, 6.0, ((1, 32),), jnp.float32),
    }


def standardize(block, freq):
    values = block.astype(jnp.float32)
    scale = lax.rsqrt(2.0 * freq * (1.0 - freq))
    return jnp.where(block < 3, (values - 2.0 * freq) * scale, jnp.float32(0.0)).astype(jnp.bfloat16)

def rounded(rows):
    return lax.optimization_barrier(rows.astype(jnp.bfloat16)).astype(jnp.float32)

def orthonormal(rows, count):
    gram = jnp.dot(rows, rows.T, precision=lax.Precision.HIGHEST) / count
    lower = jnp.linalg.cholesky(gram)
    return jax.scipy.linalg.solve_triangular(lower, rows, lower=True)

def reference(genotypes, frequency, seed_matrix):
    samples = genotypes.shape[0]
    blocks = genotypes.shape[1] // M_DEV
    geno_blocks = genotypes.reshape(samples, blocks, M_DEV).transpose(1, 0, 2)
    freq_blocks = frequency.reshape(blocks, M_DEV)

    def sample_projection(left):
        left_blocks = rounded(left).reshape(left.shape[0], blocks, M_DEV).transpose(1, 0, 2)

        def step(total, items):
            block, freq, piece = items
            xmat = standardize(block, freq).astype(jnp.float32)
            return (total + lax.dot_general(piece, xmat, (((1,), (1,)), ((), ())), precision=lax.Precision.HIGHEST), None)
        total, _ = lax.scan(step, jnp.zeros((left.shape[0], samples), jnp.float32), (geno_blocks, freq_blocks, left_blocks))
        return total

    def snp_projection(qmat):
        left = rounded(qmat)

        def step(carry, items):
            block, freq = items
            xmat = standardize(block, freq).astype(jnp.float32)
            return (carry, jnp.dot(left, xmat, precision=lax.Precision.HIGHEST))
        _, pieces = lax.scan(step, jnp.float32(0.0), (geno_blocks, freq_blocks))
        return pieces.transpose(1, 0, 2).reshape(qmat.shape[0], blocks * M_DEV)
    snps = jnp.float32(blocks * M_DEV)
    qmat = orthonormal(sample_projection(seed_matrix), jnp.float32(samples)).astype(jnp.bfloat16)
    pmat = seed_matrix.astype(jnp.bfloat16)
    for step_index in range(ITERS):
        pmat = orthonormal(snp_projection(qmat), snps).astype(jnp.bfloat16)
        qmat = orthonormal(sample_projection(pmat), jnp.float32(samples)).astype(jnp.bfloat16)
    return (qmat, pmat)
```

```python
import functools

import jax
import jax.numpy as jnp
from jax import lax
from jax.experimental import pallas as pl
from jax.experimental.pallas import tpu as pltpu
from jax.sharding import PartitionSpec as P

ITERS = 6
K = 32
LANES = 128
BLOCK = 256
EARLY = 1
MESH = pl.DeviceIdType.MESH
HIGHEST = lax.Precision.HIGHEST


def offsets(count):
    return sorted(range(count), key=lambda o: (-min(o, count - o), o))


def kernel(
    nz, ns, sample_count, snp_count,
    geno_ref, freq_ref, seed_ref, q_ref, p_ref,
    x_ref, snd_s, rcv_s, all_s, snd_z, rcv_z, all_z, gram_s, gram_z,
    load_sem, sum_s_send, sum_s_recv, all_s_send, all_s_recv,
    sum_z_send, sum_z_recv, all_z_send, all_z_recv,
    gram_s_send, gram_s_recv, gram_s_far, gram_z_send, gram_z_recv,
):
    z = lax.axis_index("samp")
    s = lax.axis_index("snp")
    chip = s // 2
    owner = lax.rem(s, 2) == 0
    rows = x_ref.shape[0]
    chips = ns // 2
    blocks_s = rows // BLOCK
    per_z = all_z.shape[0] // nz
    barrier = pltpu.get_barrier_semaphore()

    def load(block):
        part = pl.ds(pl.multiple_of(block * BLOCK, BLOCK), BLOCK)
        return pltpu.make_async_copy(geno_ref.at[part], x_ref.at[part], load_sem.at[block])

    first = chip // 2
    order_s = offsets(blocks_s)
    for off in order_s:
        load(lax.rem(first + off, blocks_s)).start()

    @pl.loop(1, ns)
    def _(d):
        pl.semaphore_signal(barrier, 1, device_id={"snp": lax.rem(s + d, ns)}, device_id_type=MESH)

    @pl.loop(1, nz)
    def _(d):
        pl.semaphore_signal(barrier, 1, device_id={"samp": lax.rem(z + d, nz)}, device_id_type=MESH)

    def send(src, dst, send_sem, recv_sem, target):
        pltpu.make_async_remote_copy(
            src_ref=src, dst_ref=dst, send_sem=send_sem, recv_sem=recv_sem,
            device_id=target, device_id_type=MESH,
        ).start()

    def settle(ref, sem):
        pltpu.make_async_copy(ref, ref, sem).wait()

    def whole(ref):
        return jnp.concatenate([ref[t] for t in range(ref.shape[0])], axis=1)

    def send_tile_s(tile):
        send(snd_s.at[tile], rcv_s.at[s], sum_s_send, sum_s_recv, {"snp": 2 * tile})

    def store_tiles(ref, block, values):
        packed = values.astype(jnp.bfloat16)
        for t in range(BLOCK // LANES):
            ref[block * (BLOCK // LANES) + t] = packed[:, t * LANES : (t + 1) * LANES]

    def product_to_samples(left, factor, prepare=None):
        pending = None
        for off in order_s:
            block = lax.rem(first + off, blocks_s)
            part = pl.ds(pl.multiple_of(block * BLOCK, BLOCK), BLOCK)
            if prepare is not None:
                prepare(block, part)
            values = lax.dot_general(
                left, x_ref[part, :], (((1,), (1,)), ((), ())), preferred_element_type=jnp.float32
            )
            if factor is not None:
                values = jnp.dot(factor, values, precision=HIGHEST, preferred_element_type=jnp.float32)
            store_tiles(snd_s, block, values)
            if pending is not None:
                send_tile_s(2 * pending)
                send_tile_s(2 * pending + 1)
            pending = block
        mate = chip + 1 - 2 * lax.rem(chip, 2)
        send_tile_s(mate)

        @pl.when(owner)
        def _():
            rcv_s[s] = snd_s[chip]

        @pl.when(jnp.logical_not(owner))
        def _():
            send_tile_s(chip)

    def sum_samples():
        settle(rcv_s.at[pl.ds(0, ns - 1)], sum_s_recv)
        total = rcv_s[0].astype(jnp.float32)
        for i in range(1, ns):
            total = total + rcv_s[i].astype(jnp.float32)
        return total

    def sent_samples():
        @pl.when(owner)
        def _():
            settle(snd_s.at[pl.ds(0, chips - 1)], sum_s_send)

        @pl.when(jnp.logical_not(owner))
        def _():
            settle(snd_s, sum_s_send)

    def share_samples(piece):
        all_s[chip] = piece.astype(jnp.bfloat16)

        @pl.loop(1, ns)
        def _(d):
            send(all_s.at[chip], all_s.at[chip], all_s_send, all_s_recv, {"snp": lax.rem(s + d, ns)})

    def await_samples():
        @pl.when(owner)
        def _():
            settle(all_s.at[pl.ds(0, chips - 1)], all_s_recv)
            settle(rcv_s.at[pl.ds(0, ns - 1)], all_s_send)

        @pl.when(jnp.logical_not(owner))
        def _():
            settle(all_s, all_s_recv)

    order_z = offsets(nz)

    def product_to_snps(left, factor):
        width = per_z * LANES
        pending = None

        def ship(block):
            part = pl.ds(block * per_z, per_z)
            send(snd_z.at[part], rcv_z.at[z], sum_z_send, sum_z_recv, {"samp": block})

        for off in order_z:
            block = lax.rem(z + off, nz)
            part = pl.ds(pl.multiple_of(block * width, width), width)
            values = jnp.dot(left, x_ref[:, part], preferred_element_type=jnp.float32)
            if factor is not None:
                values = jnp.dot(factor, values, precision=HIGHEST, preferred_element_type=jnp.float32)
            packed = values.astype(jnp.bfloat16)
            for t in range(per_z):
                tile = packed[:, t * LANES : (t + 1) * LANES]
                if off == 0:
                    rcv_z[z, t] = tile
                else:
                    snd_z[block * per_z + t] = tile
            if pending is not None:
                ship(pending)
            pending = block

    def sum_snps():
        settle(rcv_z.at[pl.ds(0, nz - 1)], sum_z_recv)
        total = rcv_z[0].astype(jnp.float32)
        for i in range(1, nz):
            total = total + rcv_z[i].astype(jnp.float32)
        return jnp.concatenate([total[t] for t in range(per_z)], axis=1)

    def share_snps(piece):
        packed = piece.astype(jnp.bfloat16)
        for t in range(per_z):
            all_z[z * per_z + t] = packed[:, t * LANES : (t + 1) * LANES]
        part = pl.ds(z * per_z, per_z)

        for off in order_z[:-1]:
            send(all_z.at[part], all_z.at[part], all_z_send, all_z_recv, {"samp": lax.rem(z + off, nz)})

    def await_snps():
        others = pl.ds(0, (nz - 1) * per_z)
        settle(all_z.at[others], all_z_recv)
        settle(all_z.at[others], all_z_send)
        settle(snd_z.at[others], sum_z_send)

    def packed_gram(left):
        four = jnp.concatenate([left] * 4, axis=0)
        wide = lax.dot_general(left, four, (((1,), (1,)), ((), ())), preferred_element_type=jnp.float32)
        band = lax.broadcasted_iota(jnp.int32, (8, LANES), 1) // K
        out = wide[0:8]
        for b in range(1, 4):
            out = jnp.where(band == b, wide[8 * b : 8 * b + 8], out)
        return out

    def send_gram_z(left):
        gram_z[z] = packed_gram(left)
        for off in order_z[:-1]:
            send(gram_z.at[z], gram_z.at[z], gram_z_send, gram_z_recv, {"samp": lax.rem(z + off, nz)})

    def take_gram_z():
        settle(gram_z.at[pl.ds(0, nz - 1)], gram_z_recv)
        settle(gram_z.at[pl.ds(0, nz - 1)], gram_z_send)
        total = gram_z[0]
        for i in range(1, nz):
            total = total + gram_z[i]
        return inverse_factor(total * (1.0 / sample_count))

    def send_gram_s(left, everyone):
        gram_s[s] = packed_gram(left)

        @pl.loop(1, chips)
        def _(d):
            send(gram_s.at[s], gram_s.at[s], gram_s_send, gram_s_recv, {"snp": 2 * lax.rem(chip + d, chips)})

        @pl.when(jnp.logical_not(owner))
        def _():
            send(gram_s.at[s], gram_s.at[s], gram_s_send, gram_s_recv, {"snp": s - 1})

        @pl.when(everyone)
        def _():
            @pl.loop(1, chips)
            def _(d):
                send(gram_s.at[s], gram_s.at[s], gram_s_far, gram_s_recv, {"snp": 2 * lax.rem(chip + d, chips) + 1})

            @pl.when(owner)
            def _():
                send(gram_s.at[s], gram_s.at[s], gram_s_far, gram_s_recv, {"snp": s + 1})

    def sent_gram_s(everyone):
        @pl.when(owner)
        def _():
            settle(gram_s.at[pl.ds(0, chips - 1)], gram_s_send)

        @pl.when(jnp.logical_not(owner))
        def _():
            settle(gram_s.at[pl.ds(0, chips)], gram_s_send)

        @pl.when(jnp.logical_and(everyone, owner))
        def _():
            settle(gram_s.at[pl.ds(0, chips)], gram_s_far)

        @pl.when(jnp.logical_and(everyone, jnp.logical_not(owner)))
        def _():
            settle(gram_s.at[pl.ds(0, chips - 1)], gram_s_far)

    def take_gram_s():
        settle(gram_s.at[pl.ds(0, ns - 1)], gram_s_recv)
        total = gram_s[0]
        for i in range(1, ns):
            total = total + gram_s[i]
        return inverse_factor(total * (1.0 / snp_count))

    def inverse_factor(packed):
        lane = lax.broadcasted_iota(jnp.int32, (K, LANES), 1)
        row = lax.broadcasted_iota(jnp.int32, (K, LANES), 0)
        bands = [pltpu.roll(packed, (K - K * b) % LANES, 1) for b in range(4)]
        mat = jnp.where(lane == row, 1.0, jnp.concatenate(bands, axis=0))
        mat = jnp.where(jnp.logical_and(lane < K, lane != row), 0.0, mat)
        for j in range(K - 1):
            line = mat[j : j + 1, :]
            column = mat[:, K + j : K + j + 1]
            share = column * (1.0 / line[:, K + j : K + j + 1])
            mat = mat - jnp.where(row > j, share, 0.0) * line
        diagonal = jnp.sum(jnp.where(lane == row + K, mat, 0.0), axis=1, keepdims=True)
        return (mat * lax.rsqrt(diagonal))[:, :K]

    def apply(factor, values):
        return jnp.dot(factor, values, precision=HIGHEST, preferred_element_type=jnp.float32)

    double = 2.0 * freq_ref[...]
    scale = lax.rsqrt(double * (1.0 - freq_ref[...]))

    def prepare(block, part):
        load(block).wait()

        @pl.loop(0, BLOCK // 32)
        def _(i):
            lines = pl.ds(pl.multiple_of(block * BLOCK + i * 32, 32), 32)
            values = x_ref[lines, :].astype(jnp.float32)
            x_ref[lines, :] = jnp.where(values < 3.0, (values - double) * scale, 0.0).astype(jnp.bfloat16)

    for off in order_s:
        block = lax.rem(first + off, blocks_s)
        prepare(block, None)
    pl.semaphore_wait(barrier, ns - 1 + nz - 1)

    def finish_samples(factor):
        @pl.when(owner)
        def _():
            total = sum_samples()
            share_samples(total if factor is None else apply(factor(), total))

        sent_samples()

    product_to_samples(seed_ref[...].astype(jnp.bfloat16), None)
    finish_samples(None)
    await_samples()

    def first_round():
        left = whole(all_s)
        send_gram_z(left)
        product_to_snps(left, take_gram_z())
        share_snps(sum_snps())
        await_snps()

    def early_samples():
        left = whole(all_z)
        send_gram_s(left, True)
        factor = take_gram_s()
        sent_gram_s(True)
        product_to_samples(left, factor)
        finish_samples(None)
        await_samples()

    def to_snps():
        left = whole(all_s)
        send_gram_z(left)
        product_to_snps(left, None)
        factor = take_gram_z()
        share_snps(apply(factor, sum_snps()))
        await_snps()

    def to_samples(last):
        left = whole(all_z)
        send_gram_s(left, last)
        product_to_samples(left, None)
        finish_samples(take_gram_s)

        @pl.when(last)
        def _():
            @pl.when(jnp.logical_not(owner))
            def _():
                settle(gram_s.at[pl.ds(0, ns - 1)], gram_s_recv)

            total = gram_s[0]
            for i in range(1, ns):
                total = total + gram_s[i]
            factor = inverse_factor(total * (1.0 / snp_count))
            p_ref[...] = apply(factor, whole(all_z).astype(jnp.float32)).astype(jnp.bfloat16)

        sent_gram_s(last)
        await_samples()

    first_round()
    if EARLY > 1:
        early_samples()
    else:
        to_samples(False)

    @pl.loop(1, ITERS)
    def _(i):
        to_snps()
        to_samples(i == ITERS - 1)

    left = whole(all_s)
    send_gram_z(left)
    q_ref[...] = apply(take_gram_z(), left.astype(jnp.float32)).astype(jnp.bfloat16)


def per_device(nz, ns, genotypes, frequency, seed_matrix):
    samples, snps = genotypes.shape
    tiles_s, tiles_z = samples // LANES, snps // LANES
    bf16, f32 = jnp.bfloat16, jnp.float32
    vmem = pl.BlockSpec(memory_space=pltpu.VMEM)
    dma = pltpu.SemaphoreType.DMA
    return pl.pallas_call(
        functools.partial(kernel, nz, ns, float(samples * nz), float(snps * ns)),
        out_shape=(
            jax.ShapeDtypeStruct((K, samples), bf16),
            jax.ShapeDtypeStruct((K, snps), bf16),
        ),
        in_specs=[pl.BlockSpec(memory_space=pl.ANY), vmem, vmem],
        out_specs=(vmem, vmem),
        scratch_shapes=[
            pltpu.VMEM((samples, snps), bf16),
            pltpu.VMEM((tiles_s, K, LANES), bf16),
            pltpu.VMEM((ns, K, LANES), bf16),
            pltpu.VMEM((tiles_s, K, LANES), bf16),
            pltpu.VMEM((tiles_z, K, LANES), bf16),
            pltpu.VMEM((nz, tiles_z // nz, K, LANES), bf16),
            pltpu.VMEM((tiles_z, K, LANES), bf16),
            pltpu.VMEM((ns, 8, LANES), f32),
            pltpu.VMEM((nz, 8, LANES), f32),
            dma((samples // BLOCK,)),
        ]
        + [dma(())] * 13,
        compiler_params=pltpu.CompilerParams(
            collective_id=0, has_side_effects=True, vmem_limit_bytes=48 * 1024 * 1024
        ),
    )(genotypes, frequency.reshape(1, snps), seed_matrix)


def solution(mesh):
    placed = (P("samp", "snp"), P("snp"), P(None, "snp"))
    return jax.shard_map(
        functools.partial(per_device, mesh.shape["samp"], mesh.shape["snp"]),
        mesh=mesh,
        in_specs=placed,
        out_specs=(P(None, "samp"), P(None, "snp")),
        check_vma=False,
    )
```

```python
import functools
import math

import jax
import jax.numpy as jnp
from jax import lax
from jax.experimental import pallas as pl
from jax.experimental.pallas import tpu as pltpu
from jax.sharding import PartitionSpec as P

ITERS = 6
K = 32
LANES = 128
BLOCK = 256
PANEL = 8
MESH = pl.DeviceIdType.MESH
HIGHEST = lax.Precision.HIGHEST


def hops(offset, count):
    return min(offset, count - offset)


def apply(factor, values):
    return jnp.dot(factor, values, precision=HIGHEST, preferred_element_type=jnp.float32)


def packed_gram(wide):
    band = lax.broadcasted_iota(jnp.int32, (8, LANES), 1) // K
    out = wide[0:8]
    for b in range(1, 4):
        out = jnp.where(band == b, wide[8 * b : 8 * b + 8], out)
    return out


def inverse_factor(packed):
    lane = lax.broadcasted_iota(jnp.int32, (8, LANES), 1)
    row = lax.broadcasted_iota(jnp.int32, (8, LANES), 0)
    bands = []
    for b in range(4):
        shift = (K - K * b) % LANES
        band = pltpu.roll(packed, shift, 1) if shift else packed
        bands.append(jnp.where(lane < K, jnp.where(lane == row + 8 * b, 1.0, 0.0), band))
    for p in range(K // PANEL):
        start = K + PANEL * p
        columns = [
            [jnp.broadcast_to(bands[b][:, start + c : start + c + 1], (8, LANES)) for b in range(p, 4)]
            for c in range(PANEL)
        ]
        for c in range(PANEL):
            inverse = 1.0 / columns[c][0][c : c + 1, :]
            line = bands[p][c : c + 1, :] * inverse
            heads = [columns[d][0][c : c + 1, :] * inverse for d in range(c + 1, PANEL)]
            for b in range(p, 4):
                share = columns[c][b - p]
                if b == p:
                    share = jnp.where(row > c, share, 0.0)
                bands[b] = bands[b] - share * line
                for d in range(c + 1, PANEL):
                    columns[d][b - p] = columns[d][b - p] - share * heads[d - c - 1]
    out = []
    for b in range(4):
        diagonal = jnp.sum(jnp.where(lane == row + K + 8 * b, bands[b], 0.0), axis=1, keepdims=True)
        out.append(bands[b] * lax.rsqrt(diagonal))
    return jnp.concatenate(out, axis=0)[:, :K]


def kernel(
    nz, ns, sample_count, snp_count,
    geno_ref, freq_ref, seed_ref, q_ref, p_ref,
    x_ref, acc_ref, snd_s, rcv_s, all_s, snd_z, rcv_z, all_z, gram_s, gram_z,
    load_sem, all_s_recv, all_z_recv, sum_s_send, sum_s_recv, all_s_send,
    sum_z_send, sum_z_recv, all_z_send,
    gram_s_send, gram_s_recv, gram_s_far, gram_z_send, gram_z_recv,
):
    z = lax.axis_index("samp")
    s = lax.axis_index("snp")
    chip = s // 2
    owner = lax.rem(s, 2) == 0
    rows = x_ref.shape[0]
    chips = ns // 2
    side = math.isqrt(chips)
    halves = side // 2
    x, y = chip // side, lax.rem(chip, side)
    half = y // 2
    barrier = pltpu.get_barrier_semaphore()
    per_block = BLOCK // LANES

    near_s = sorted(
        ((dx, dh) for dx in range(side) for dh in range(halves)), key=lambda o: (hops(o[0], side) + o[1], o)
    )
    near_z = sorted(range(nz), key=lambda o: (hops(o, nz), o))
    places = sorted(
        ((dx, dy, dc) for dx in range(side) for dy in range(side) for dc in range(2)),
        key=lambda o: (-hops(o[0], side) - hops(o[1], side), o),
    )

    def block_s(offset):
        return lax.rem(x + offset[0], side) * halves + lax.rem(half + offset[1], halves)

    def place_s(offset):
        return (lax.rem(x + offset[0], side) * side + lax.rem(y + offset[1], side)) * 2

    def place_z(offset):
        return lax.rem(z + offset, nz)

    def span(block):
        return pl.ds(pl.multiple_of(block * BLOCK, BLOCK), BLOCK)

    def load(block):
        return pltpu.make_async_copy(geno_ref.at[span(block)], x_ref.at[span(block)], load_sem.at[block])

    for offset in reversed(near_s):
        load(block_s(offset)).start()

    @pl.loop(1, ns)
    def _(d):
        pl.semaphore_signal(barrier, 1, device_id={"snp": lax.rem(s + d, ns)}, device_id_type=MESH)

    @pl.loop(1, nz)
    def _(d):
        pl.semaphore_signal(barrier, 1, device_id={"samp": lax.rem(z + d, nz)}, device_id_type=MESH)

    def send(src, dst, send_sem, recv_sem, target):
        pltpu.make_async_remote_copy(
            src_ref=src, dst_ref=dst, send_sem=send_sem, recv_sem=recv_sem,
            device_id=target, device_id_type=MESH,
        ).start()

    def settle(ref, sem):
        pltpu.make_async_copy(ref, ref, sem).wait()

    def two(ref, block):
        return jnp.concatenate([ref[block * per_block + t] for t in range(per_block)], axis=1)

    def whole(ref):
        return jnp.concatenate([ref[t] for t in range(ref.shape[0])], axis=1)

    def band_product(left):
        four = jnp.concatenate([left] * 4, axis=0)
        return lax.dot_general(left, four, (((1,), (1,)), ((), ())), preferred_element_type=jnp.float32)

    def times_xt(left, lines, columns):
        return lax.dot_general(
            left, x_ref[lines, columns], (((1,), (1,)), ((), ())), preferred_element_type=jnp.float32
        )

    def times_x(left, lines, columns):
        return jnp.dot(left, x_ref[lines, columns], preferred_element_type=jnp.float32)


    def send_tile_s(tile):
        send(snd_s.at[tile], rcv_s.at[s], sum_s_send, sum_s_recv, {"snp": 2 * tile})

    def ship_s(product):
        pending = None
        for offset in reversed(near_s):
            block = block_s(offset)
            packed = product(block).astype(jnp.bfloat16)
            for t in range(per_block):
                snd_s[block * per_block + t] = packed[:, t * LANES : (t + 1) * LANES]
            if pending is not None:
                for t in range(per_block):
                    send_tile_s(pending * per_block + t)
            pending = block
        send_tile_s(chip + 1 - 2 * lax.rem(chip, 2))

        @pl.when(owner)
        def _():
            rcv_s[s] = snd_s[chip]

        @pl.when(jnp.logical_not(owner))
        def _():
            send_tile_s(chip)

    def finish_samples(factor):
        @pl.when(owner)
        def _():
            inverse = None if factor is None else factor()
            settle(rcv_s.at[pl.ds(0, ns - 1)], sum_s_recv)
            total = rcv_s[0].astype(jnp.float32)
            for i in range(1, ns):
                total = total + rcv_s[i].astype(jnp.float32)
            if inverse is not None:
                total = apply(inverse, total)
            all_s[chip] = total.astype(jnp.bfloat16)
            for offset in places:
                if offset == (0, 0, 0):
                    continue
                target = {"snp": place_s(offset) + offset[2]}
                send(all_s.at[chip], all_s.at[chip], all_s_send, all_s_recv.at[chip // 2], target)
            settle(snd_s.at[pl.ds(0, chips - 1)], sum_s_send)

        @pl.when(jnp.logical_not(owner))
        def _():
            settle(snd_s, sum_s_send)

    def await_block_s(offset):
        block = block_s(offset)
        if offset == (0, 0):
            @pl.when(owner)
            def _():
                settle(all_s.at[pl.ds(0, 1)], all_s_recv.at[block])

            @pl.when(jnp.logical_not(owner))
            def _():
                settle(all_s.at[pl.ds(0, 2)], all_s_recv.at[block])
        else:
            settle(all_s.at[pl.ds(0, 2)], all_s_recv.at[block])
        return block

    def sent_all_s():
        @pl.when(owner)
        def _():
            settle(rcv_s.at[pl.ds(0, ns - 1)], all_s_send)


    def ship_z(product):
        pending = None

        def ship(block):
            part = pl.ds(block * per_block, per_block)
            send(snd_z.at[part], rcv_z.at[z], sum_z_send, sum_z_recv, {"samp": block})

        for offset in reversed(near_z):
            block = place_z(offset)
            packed = product(block).astype(jnp.bfloat16)
            for t in range(per_block):
                tile = packed[:, t * LANES : (t + 1) * LANES]
                if offset == 0:
                    rcv_z[z, t] = tile
                else:
                    snd_z[block * per_block + t] = tile
            if pending is not None:
                ship(pending)
            pending = block

    def finish_snps(inverse):
        others = pl.ds(0, (nz - 1) * per_block)
        settle(rcv_z.at[pl.ds(0, nz - 1)], sum_z_recv)
        total = rcv_z[0].astype(jnp.float32)
        for i in range(1, nz):
            total = total + rcv_z[i].astype(jnp.float32)
        total = apply(inverse, jnp.concatenate([total[t] for t in range(per_block)], axis=1))
        packed = total.astype(jnp.bfloat16)
        for t in range(per_block):
            all_z[z * per_block + t] = packed[:, t * LANES : (t + 1) * LANES]
        part = pl.ds(z * per_block, per_block)
        for offset in reversed(near_z[1:]):
            send(
                all_z.at[part], all_z.at[part], all_z_send, all_z_recv.at[nz - offset],
                {"samp": place_z(offset)},
            )
        settle(snd_z.at[others], sum_z_send)

    def await_block_z(offset):
        if offset != 0:
            settle(all_z.at[pl.ds(0, per_block)], all_z_recv.at[offset])
        return place_z(offset)

    def sent_all_z():
        settle(all_z.at[pl.ds(0, (nz - 1) * per_block)], all_z_send)


    def send_gram_z(wide):
        gram_z[z] = packed_gram(wide)
        for offset in reversed(near_z[1:]):
            send(gram_z.at[z], gram_z.at[z], gram_z_send, gram_z_recv, {"samp": place_z(offset)})

    def take_gram_z():
        settle(gram_z.at[pl.ds(0, nz - 1)], gram_z_recv)
        settle(gram_z.at[pl.ds(0, nz - 1)], gram_z_send)
        total = gram_z[0]
        for i in range(1, nz):
            total = total + gram_z[i]
        return inverse_factor(total * (1.0 / sample_count))

    def send_gram_s(wide, everyone):
        gram_s[s] = packed_gram(wide)
        for offset in places:
            if offset[2] == 0 and offset != (0, 0, 0):
                send(gram_s.at[s], gram_s.at[s], gram_s_send, gram_s_recv, {"snp": place_s(offset)})

        @pl.when(jnp.logical_not(owner))
        def _():
            send(gram_s.at[s], gram_s.at[s], gram_s_send, gram_s_recv, {"snp": s - 1})

        @pl.when(everyone)
        def _():
            @pl.loop(1, chips)
            def _(d):
                send(gram_s.at[s], gram_s.at[s], gram_s_far, gram_s_recv, {"snp": 2 * lax.rem(chip + d, chips) + 1})

            @pl.when(owner)
            def _():
                send(gram_s.at[s], gram_s.at[s], gram_s_far, gram_s_recv, {"snp": s + 1})

    def sent_gram_s(everyone):
        @pl.when(owner)
        def _():
            settle(gram_s.at[pl.ds(0, chips - 1)], gram_s_send)

        @pl.when(jnp.logical_not(owner))
        def _():
            settle(gram_s.at[pl.ds(0, chips)], gram_s_send)

        @pl.when(jnp.logical_and(everyone, owner))
        def _():
            settle(gram_s.at[pl.ds(0, chips)], gram_s_far)

        @pl.when(jnp.logical_and(everyone, jnp.logical_not(owner)))
        def _():
            settle(gram_s.at[pl.ds(0, chips - 1)], gram_s_far)

    def factor_s():
        total = gram_s[0]
        for i in range(1, ns):
            total = total + gram_s[i]
        return inverse_factor(total * (1.0 / snp_count))

    def take_gram_s():
        settle(gram_s.at[pl.ds(0, ns - 1)], gram_s_recv)
        return factor_s()

    double = 2.0 * freq_ref[...]
    scale = lax.rsqrt(double * (1.0 - freq_ref[...]))
    for offset in reversed(near_s):
        block = block_s(offset)
        load(block).wait()

        @pl.loop(0, BLOCK // 32)
        def _(i):
            lines = pl.ds(pl.multiple_of(block * BLOCK + i * 32, 32), 32)
            values = x_ref[lines, :].astype(jnp.float32)
            x_ref[lines, :] = jnp.where(values < 3.0, (values - double) * scale, 0.0).astype(jnp.bfloat16)

    pl.semaphore_wait(barrier, ns - 1 + nz - 1)
    every = slice(None)
    seed = seed_ref[...].astype(jnp.bfloat16)
    ship_s(lambda block: times_xt(seed, span(block), every))
    finish_samples(None)

    def to_snps():
        wide = None
        for i, offset in enumerate(near_s):
            block = await_block_s(offset)
            left = two(all_s, block)
            part = band_product(left)
            wide = part if wide is None else wide + part
            if i < len(near_s) - 1:
                values = times_x(left, span(block), every)
                acc_ref[...] = values if i == 0 else acc_ref[...] + values
        send_gram_z(wide)
        ship_z(lambda out: acc_ref[:, span(out)] + times_x(left, span(block), span(out)))
        sent_all_s()
        finish_snps(take_gram_z())

    def to_samples(last):
        wide = None
        for i, offset in enumerate(near_z):
            block = await_block_z(offset)
            left = two(all_z, block)
            part = band_product(left)
            wide = part if wide is None else wide + part
            if i < len(near_z) - 1:
                values = times_xt(left, every, span(block))
                acc_ref[...] = values if i == 0 else acc_ref[...] + values
        send_gram_s(wide, last)
        ship_s(lambda out: acc_ref[:, span(out)] + times_xt(left, span(out), span(block)))
        sent_all_z()
        finish_samples(take_gram_s)

        @pl.when(last)
        def _():
            @pl.when(jnp.logical_not(owner))
            def _():
                settle(gram_s.at[pl.ds(0, ns - 1)], gram_s_recv)

            p_ref[...] = apply(factor_s(), whole(all_z).astype(jnp.float32)).astype(jnp.bfloat16)

        sent_gram_s(last)

    @pl.loop(0, ITERS)
    def _(i):
        to_snps()
        to_samples(i == ITERS - 1)

    wide = None
    for offset in near_s:
        part = band_product(two(all_s, await_block_s(offset)))
        wide = part if wide is None else wide + part
    send_gram_z(wide)
    sent_all_s()
    q_ref[...] = apply(take_gram_z(), whole(all_s).astype(jnp.float32)).astype(jnp.bfloat16)


def per_device(nz, ns, genotypes, frequency, seed_matrix):
    samples, snps = genotypes.shape
    tiles_s, tiles_z = samples // LANES, snps // LANES
    bf16, f32 = jnp.bfloat16, jnp.float32
    vmem = pl.BlockSpec(memory_space=pltpu.VMEM)
    dma = pltpu.SemaphoreType.DMA
    return pl.pallas_call(
        functools.partial(kernel, nz, ns, float(samples * nz), float(snps * ns)),
        out_shape=(
            jax.ShapeDtypeStruct((K, samples), bf16),
            jax.ShapeDtypeStruct((K, snps), bf16),
        ),
        in_specs=[pl.BlockSpec(memory_space=pl.ANY), vmem, vmem],
        out_specs=(vmem, vmem),
        scratch_shapes=[
            pltpu.VMEM((samples, snps), bf16),
            pltpu.VMEM((K, max(samples, snps)), f32),
            pltpu.VMEM((tiles_s, K, LANES), bf16),
            pltpu.VMEM((ns, K, LANES), bf16),
            pltpu.VMEM((tiles_s, K, LANES), bf16),
            pltpu.VMEM((tiles_z, K, LANES), bf16),
            pltpu.VMEM((nz, tiles_z // nz, K, LANES), bf16),
            pltpu.VMEM((tiles_z, K, LANES), bf16),
            pltpu.VMEM((ns, 8, LANES), f32),
            pltpu.VMEM((nz, 8, LANES), f32),
            dma((samples // BLOCK,)),
            dma((samples // BLOCK,)),
            dma((nz,)),
        ]
        + [dma(())] * 11,
        compiler_params=pltpu.CompilerParams(
            collective_id=0, has_side_effects=True, vmem_limit_bytes=48 * 1024 * 1024
        ),
    )(genotypes, frequency.reshape(1, snps), seed_matrix)


def solution(mesh):
    placed = (P("samp", "snp"), P("snp"), P(None, "snp"))
    return jax.shard_map(
        functools.partial(per_device, mesh.shape["samp"], mesh.shape["snp"]),
        mesh=mesh,
        in_specs=placed,
        out_specs=(P(None, "samp"), P(None, "snp")),
        check_vma=False,
    )
```

```python
import functools
import math

import jax
import jax.numpy as jnp
from jax import lax
from jax.experimental import pallas as pl
from jax.experimental.pallas import tpu as pltpu
from jax.sharding import PartitionSpec as P

ITERS = 6
K = 32
LANES = 128
BLOCK = 256
PANEL = 8
MESH = pl.DeviceIdType.MESH
HALF = K // 2


def hops(offset, count):
    return min(offset, count - offset)


def in_parts(factor):
    high = factor.astype(jnp.bfloat16)
    rest = factor - high.astype(jnp.float32)
    middle = rest.astype(jnp.bfloat16)
    low = (rest - middle.astype(jnp.float32)).astype(jnp.bfloat16)
    return jnp.concatenate([high, middle, low], axis=0)


def apply(parts, values):
    three = jnp.dot(parts, values, preferred_element_type=jnp.float32)
    return (three[:K] + three[K : 2 * K] + three[2 * K :]).astype(jnp.bfloat16)


def packed_gram(wide):
    band = lax.broadcasted_iota(jnp.int32, (8, LANES), 1) // K
    out = wide[0:8]
    for b in range(1, 4):
        out = jnp.where(band == b, wide[8 * b : 8 * b + 8], out)
    return out


def inverse_factor(packed):
    lane = lax.broadcasted_iota(jnp.int32, (8, LANES), 1)
    row = lax.broadcasted_iota(jnp.int32, (8, LANES), 0)
    bands = []
    for b in range(4):
        shift = (K - K * b) % LANES
        band = pltpu.roll(packed, shift, 1) if shift else packed
        bands.append(jnp.where(lane < K, jnp.where(lane == row + 8 * b, 1.0, 0.0), band))
    for p in range(K // PANEL):
        start = K + PANEL * p
        columns = [
            [jnp.broadcast_to(bands[b][:, start + c : start + c + 1], (8, LANES)) for b in range(p, 4)]
            for c in range(PANEL)
        ]
        for c in range(PANEL):
            inverse = 1.0 / columns[c][0][c : c + 1, :]
            line = bands[p][c : c + 1, :] * inverse
            heads = [columns[d][0][c : c + 1, :] * inverse for d in range(c + 1, PANEL)]
            for b in range(p, 4):
                share = columns[c][b - p]
                if b == p:
                    share = jnp.where(row > c, share, 0.0)
                bands[b] = bands[b] - share * line
                for d in range(c + 1, PANEL):
                    columns[d][b - p] = columns[d][b - p] - share * heads[d - c - 1]
    out = []
    for b in range(4):
        diagonal = jnp.sum(jnp.where(lane == row + K + 8 * b, bands[b], 0.0), axis=1, keepdims=True)
        out.append(bands[b] * lax.rsqrt(diagonal))
    return jnp.concatenate(out, axis=0)[:, :K]


def kernel(
    nz, ns, sample_count, snp_count,
    geno_ref, freq_ref, seed_ref, q_ref, p_ref,
    x_ref, acc_ref, factor_ref, frequency_ref, start_ref,
    snd_s, rcv_s, all_s, snd_z, rcv_z, all_z, gram_s, gram_z, mine_ref, mate_ref,
    load_sem, all_s_recv, all_z_recv, gram_s_recv, gram_z_recv, mate_recv,
    freq_sem, seed_sem, sum_s_send, sum_s_recv, all_s_send,
    sum_z_send, sum_z_recv, all_z_send, gram_s_send, gram_z_send, mate_send,
):
    z = lax.axis_index("samp")
    s = lax.axis_index("snp")
    chip, core = s // 2, lax.rem(s, 2)
    chips = ns // 2
    side = math.isqrt(chips)
    halves = side // 2
    x, y = chip // side, lax.rem(chip, side)
    half = y // 2
    barrier = pltpu.get_barrier_semaphore()
    per_block = BLOCK // LANES
    owners = 2 * per_block
    every = slice(None)

    near_s = sorted(
        ((dx, dh) for dx in range(side) for dh in range(halves)), key=lambda o: (hops(o[0], side) + o[1], o)
    )
    near_z = sorted(range(nz), key=lambda o: (hops(o, nz), o))
    places = sorted(
        ((dx, dy, dc) for dx in range(side) for dy in range(side) for dc in range(2)),
        key=lambda o: (-hops(o[0], side) - hops(o[1], side), o),
    )
    places.remove((0, 0, 0))

    def block_s(offset):
        return lax.rem(x + offset[0], side) * halves + lax.rem(half + offset[1], halves)

    def chip_s(offset):
        return lax.rem(x + offset[0], side) * side + lax.rem(y + offset[1], side)

    def place_s(offset):
        return chip_s(offset) * 2 + lax.rem(core + offset[2], 2)

    def place_z(offset):
        return lax.rem(z + offset, nz)

    def span(block):
        return pl.ds(pl.multiple_of(block * BLOCK, BLOCK), BLOCK)

    def load(block):
        return pltpu.make_async_copy(geno_ref.at[span(block)], x_ref.at[span(block)], load_sem.at[block])

    load_freq = pltpu.make_async_copy(freq_ref, frequency_ref, freq_sem)
    load_seed = pltpu.make_async_copy(seed_ref, start_ref, seed_sem)
    load_freq.start()
    for offset in reversed(near_s):
        load(block_s(offset)).start()
    load_seed.start()

    @pl.loop(1, ns)
    def _(d):
        pl.semaphore_signal(barrier, 1, device_id={"snp": lax.rem(s + d, ns)}, device_id_type=MESH)

    @pl.loop(1, nz)
    def _(d):
        pl.semaphore_signal(barrier, 1, device_id={"samp": lax.rem(z + d, nz)}, device_id_type=MESH)

    def send(src, dst, send_sem, recv_sem, target):
        pltpu.make_async_remote_copy(
            src_ref=src, dst_ref=dst, send_sem=send_sem, recv_sem=recv_sem,
            device_id=target, device_id_type=MESH,
        ).start()

    def settle(ref, sem):
        pltpu.make_async_copy(ref, ref, sem).wait()

    def band_product(left):
        four = jnp.concatenate([left] * 4, axis=0)
        return lax.dot_general(left, four, (((1,), (1,)), ((), ())), preferred_element_type=jnp.float32)

    def times_xt(left, lines, columns):
        return lax.dot_general(
            left, x_ref[lines, columns], (((1,), (1,)), ((), ())), preferred_element_type=jnp.float32
        )

    def times_x(left, lines, columns):
        return jnp.dot(left, x_ref[lines, columns], preferred_element_type=jnp.float32)


    others_s = pl.ds(0, ns - 1)

    def ship_s(product):
        pending = None
        for offset in reversed(near_s):
            block = block_s(offset)
            packed = product(block).astype(jnp.bfloat16)
            for t in range(owners):
                column = (t // 2) * LANES
                snd_s[block * owners + t] = packed[HALF * (t % 2) : HALF * (t % 2 + 1), column : column + LANES]
            if pending is not None:
                for t in range(owners):
                    tile = pending * owners + t
                    send(snd_s.at[tile], rcv_s.at[s], sum_s_send, sum_s_recv, {"snp": tile})
            pending = block
        for t in range(1, owners):
            tile = pending * owners + lax.rem(lax.rem(s, owners) + t, owners)
            send(snd_s.at[tile], rcv_s.at[s], sum_s_send, sum_s_recv, {"snp": tile})
        rcv_s[s] = snd_s[s]

    def finish_samples():
        settle(rcv_s.at[others_s], sum_s_recv)
        total = rcv_s[0].astype(jnp.float32)
        for i in range(1, ns):
            total = total + rcv_s[i].astype(jnp.float32)
        all_s[s] = total.astype(jnp.bfloat16)
        for offset in places:
            send(all_s.at[s], all_s.at[s], all_s_send, all_s_recv.at[chip // 2], {"snp": place_s(offset)})
        settle(snd_s.at[others_s], sum_s_send)

    def take_block_s(offset):
        block = block_s(offset)
        settle(all_s.at[pl.ds(0, owners - (offset == (0, 0)))], all_s_recv.at[block])
        columns = [
            jnp.concatenate([all_s[block * owners + 2 * t], all_s[block * owners + 2 * t + 1]], axis=0)
            for t in range(per_block)
        ]
        values = apply(factor_ref[...], jnp.concatenate(columns, axis=1))
        q_ref[:, span(block)] = values
        return block, values


    others_z = pl.ds(0, nz - 1)
    other_tiles_z = pl.ds(0, (nz - 1) * per_block)

    def ship_z(product):
        pending = None

        def ship(block):
            part = pl.ds(block * per_block, per_block)
            send(snd_z.at[part], rcv_z.at[z], sum_z_send, sum_z_recv, {"samp": block})

        for offset in reversed(near_z):
            block = place_z(offset)
            packed = product(block).astype(jnp.bfloat16)
            for t in range(per_block):
                tile = packed[:, t * LANES : (t + 1) * LANES]
                if offset == 0:
                    rcv_z[z, t] = tile
                else:
                    snd_z[block * per_block + t] = tile
            if pending is not None:
                ship(pending)
            pending = block

    def finish_snps():
        settle(rcv_z.at[others_z], sum_z_recv)
        total = rcv_z[0].astype(jnp.float32)
        for i in range(1, nz):
            total = total + rcv_z[i].astype(jnp.float32)
        part = pl.ds(z * per_block, per_block)
        all_z[part] = total.astype(jnp.bfloat16)
        for offset in reversed(near_z[1:]):
            send(
                all_z.at[part], all_z.at[part], all_z_send, all_z_recv.at[nz - offset],
                {"samp": place_z(offset)},
            )
        settle(snd_z.at[other_tiles_z], sum_z_send)

    def take_block_z(offset):
        block = place_z(offset)
        if offset != 0:
            settle(all_z.at[pl.ds(0, per_block)], all_z_recv.at[offset])
        tiles = [all_z[block * per_block + t] for t in range(per_block)]
        values = apply(factor_ref[...], jnp.concatenate(tiles, axis=1))
        p_ref[:, span(block)] = values
        return block, values


    def send_gram_z(turn, wide):
        gram_z[turn, z] = packed_gram(wide)
        for offset in reversed(near_z[1:]):
            mine = gram_z.at[turn, z]
            send(mine, mine, gram_z_send, gram_z_recv.at[turn], {"samp": place_z(offset)})

    def take_gram_z(turn):
        settle(gram_z.at[turn, others_z], gram_z_recv.at[turn])
        settle(gram_z.at[turn, others_z], gram_z_send)
        total = gram_z[turn, 0]
        for i in range(1, nz):
            total = total + gram_z[turn, i]
        factor_ref[...] = in_parts(inverse_factor(total * (1.0 / sample_count)))

    other_chips = pl.ds(0, chips - 1)

    def send_gram_s(turn, wide):
        gram_s[turn, chip] = packed_gram(wide)
        for offset in places:
            if offset[2] == 0:
                mine = gram_s.at[turn, chip]
                send(mine, mine, gram_s_send, gram_s_recv.at[turn], {"snp": place_s(offset)})

    def take_gram_s(turn):
        settle(gram_s.at[turn, other_chips], gram_s_recv.at[turn])
        total = gram_s[turn, 0]
        for i in range(1, chips):
            total = total + gram_s[turn, i]
        mine_ref[...] = total
        send(mine_ref, mate_ref.at[turn], mate_send, mate_recv.at[turn], {"snp": s + 1 - 2 * core})
        settle(gram_s.at[turn, other_chips], gram_s_send)
        settle(mate_ref.at[turn], mate_recv.at[turn])
        settle(mine_ref, mate_send)
        total = (total + mate_ref[turn]) * (1.0 / snp_count)
        factor_ref[...] = in_parts(inverse_factor(total))

    load_freq.wait()
    double = 2.0 * frequency_ref[...]
    scale = lax.rsqrt(double * (1.0 - frequency_ref[...]))
    levels = [((dosage - double) * scale).astype(jnp.bfloat16) for dosage in (0.0, 1.0, 2.0)]
    eye = lax.broadcasted_iota(jnp.int32, (K, K), 0) == lax.broadcasted_iota(jnp.int32, (K, K), 1)
    factor_ref[...] = in_parts(jnp.where(eye, 1.0, 0.0))

    for offset in reversed(near_s):
        block = block_s(offset)
        load(block).wait()

        @pl.loop(0, BLOCK // 32)
        def _(i):
            lines = pl.ds(pl.multiple_of(block * BLOCK + i * 32, 32), 32)
            values = x_ref[lines, :]
            known = jnp.where(
                values == 0.0, levels[0], jnp.where(values == 1.0, levels[1], levels[2])
            )
            x_ref[lines, :] = jnp.where(values < 3.0, known, jnp.bfloat16(0.0))

    load_seed.wait()
    seed = start_ref[...].astype(jnp.bfloat16)
    pl.semaphore_wait(barrier, ns - 1 + nz - 1)
    ship_s(lambda block: times_xt(seed, span(block), every))
    finish_samples()

    def to_snps(turn):
        wide = None
        for i, offset in enumerate(near_s):
            block, left = take_block_s(offset)
            part = band_product(left)
            wide = part if wide is None else wide + part
            if i < len(near_s) - 1:
                values = times_x(left, span(block), every)
                acc_ref[...] = values if i == 0 else acc_ref[...] + values
        ship_z(lambda out: acc_ref[:, span(out)] + times_x(left, span(block), span(out)))
        send_gram_z(turn, wide)
        settle(rcv_s.at[others_s], all_s_send)
        finish_snps()
        take_gram_z(turn)

    def to_samples(turn):
        wide = None
        for i, offset in enumerate(near_z):
            block, left = take_block_z(offset)
            part = band_product(left)
            wide = part if wide is None else wide + part
            if i < len(near_z) - 1:
                values = times_xt(left, every, span(block))
                acc_ref[...] = values if i == 0 else acc_ref[...] + values
        ship_s(lambda out: acc_ref[:, span(out)] + times_xt(left, span(out), span(block)))
        send_gram_s(turn, wide)
        settle(all_z.at[other_tiles_z], all_z_send)
        finish_samples()
        take_gram_s(turn)

    @pl.loop(0, ITERS)
    def _(i):
        turn = lax.rem(i, 2)
        to_snps(turn)
        to_samples(turn)

    final = ITERS % 2
    for block in range(p_ref.shape[1] // BLOCK):
        columns = slice(block * BLOCK, (block + 1) * BLOCK)
        p_ref[:, columns] = apply(factor_ref[...], p_ref[:, columns])
    wide = None
    for offset in near_s:
        part = band_product(take_block_s(offset)[1])
        wide = part if wide is None else wide + part
    send_gram_z(final, wide)
    settle(rcv_s.at[others_s], all_s_send)
    take_gram_z(final)
    for block in range(q_ref.shape[1] // BLOCK):
        columns = slice(block * BLOCK, (block + 1) * BLOCK)
        q_ref[:, columns] = apply(factor_ref[...], q_ref[:, columns])


def per_device(nz, ns, genotypes, frequency, seed_matrix):
    samples, snps = genotypes.shape
    tiles_s, tiles_z, chips = samples // LANES, snps // LANES, ns // 2
    bf16, f32 = jnp.bfloat16, jnp.float32
    vmem, hbm = pl.BlockSpec(memory_space=pltpu.VMEM), pl.BlockSpec(memory_space=pl.ANY)
    dma = pltpu.SemaphoreType.DMA
    return pl.pallas_call(
        functools.partial(kernel, nz, ns, float(samples * nz), float(snps * ns)),
        out_shape=(
            jax.ShapeDtypeStruct((K, samples), bf16),
            jax.ShapeDtypeStruct((K, snps), bf16),
        ),
        in_specs=[hbm, hbm, hbm],
        out_specs=(vmem, vmem),
        scratch_shapes=[
            pltpu.VMEM((samples, snps), bf16),
            pltpu.VMEM((K, max(samples, snps)), f32),
            pltpu.VMEM((3 * K, K), bf16),
            pltpu.VMEM((1, snps), f32),
            pltpu.VMEM((K, snps), f32),
            pltpu.VMEM((ns, HALF, LANES), bf16),
            pltpu.VMEM((ns, HALF, LANES), bf16),
            pltpu.VMEM((ns, HALF, LANES), bf16),
            pltpu.VMEM((tiles_z, K, LANES), bf16),
            pltpu.VMEM((nz, tiles_z // nz, K, LANES), bf16),
            pltpu.VMEM((tiles_z, K, LANES), bf16),
            pltpu.VMEM((2, chips, 8, LANES), f32),
            pltpu.VMEM((2, nz, 8, LANES), f32),
            pltpu.VMEM((8, LANES), f32),
            pltpu.VMEM((2, 8, LANES), f32),
            dma((samples // BLOCK,)),
            dma((samples // BLOCK,)),
            dma((nz,)),
            dma((2,)),
            dma((2,)),
            dma((2,)),
        ]
        + [dma(())] * 11,
        compiler_params=pltpu.CompilerParams(
            collective_id=0, has_side_effects=True, vmem_limit_bytes=48 * 1024 * 1024
        ),
    )(genotypes, frequency.reshape(1, snps), seed_matrix)


def solution(mesh):
    placed = (P("samp", "snp"), P("snp"), P(None, "snp"))
    return jax.shard_map(
        functools.partial(per_device, mesh.shape["samp"], mesh.shape["snp"]),
        mesh=mesh,
        in_specs=placed,
        out_specs=(P(None, "samp"), P(None, "snp")),
        check_vma=False,
    )
```

```python
import functools
import math

import jax
import jax.numpy as jnp
from jax import lax
from jax.experimental import pallas as pl
from jax.experimental.pallas import tpu as pltpu
from jax.sharding import PartitionSpec as P

ITERS = 6
K = 32
LANES = 128
BLOCK = 256
PANEL = 8
EARLY = 5
MESH = pl.DeviceIdType.MESH
HALF = K // 2


def hops(offset, count):
    return min(offset, count - offset)


def in_parts(factor):
    high = factor.astype(jnp.bfloat16)
    rest = factor - high.astype(jnp.float32)
    middle = rest.astype(jnp.bfloat16)
    low = (rest - middle.astype(jnp.float32)).astype(jnp.bfloat16)
    return jnp.concatenate([high, middle, low], axis=0)


def apply(parts, values):
    three = jnp.dot(parts, values, preferred_element_type=jnp.float32)
    return (three[:K] + three[K : 2 * K] + three[2 * K :]).astype(jnp.bfloat16)


def packed_gram(wide):
    band = lax.broadcasted_iota(jnp.int32, (8, LANES), 1) // K
    out = wide[0:8]
    for b in range(1, 4):
        out = jnp.where(band == b, wide[8 * b : 8 * b + 8], out)
    return out


def inverse_factor(packed):
    lane = lax.broadcasted_iota(jnp.int32, (8, LANES), 1)
    row = lax.broadcasted_iota(jnp.int32, (8, LANES), 0)
    bands = []
    for b in range(4):
        shift = (K - K * b) % LANES
        band = pltpu.roll(packed, shift, 1) if shift else packed
        bands.append(jnp.where(lane < K, jnp.where(lane == row + 8 * b, 1.0, 0.0), band))
    for p in range(K // PANEL):
        start = K + PANEL * p
        columns = [
            [jnp.broadcast_to(bands[b][:, start + c : start + c + 1], (8, LANES)) for b in range(p, 4)]
            for c in range(PANEL)
        ]
        for c in range(PANEL):
            inverse = 1.0 / columns[c][0][c : c + 1, :]
            line = bands[p][c : c + 1, :] * inverse
            heads = [columns[d][0][c : c + 1, :] * inverse for d in range(c + 1, PANEL)]
            for b in range(p, 4):
                share = columns[c][b - p]
                if b == p:
                    share = jnp.where(row > c, share, 0.0)
                bands[b] = bands[b] - share * line
                for d in range(c + 1, PANEL):
                    columns[d][b - p] = columns[d][b - p] - share * heads[d - c - 1]
    out = []
    for b in range(4):
        diagonal = jnp.sum(jnp.where(lane == row + K + 8 * b, bands[b], 0.0), axis=1, keepdims=True)
        out.append(bands[b] * lax.rsqrt(diagonal))
    return jnp.concatenate(out, axis=0)[:, :K]


def kernel(
    nz, ns, sample_count, snp_count,
    geno_ref, freq_ref, seed_ref, q_ref, p_ref,
    x_ref, xt_ref, acc_ref, factor_ref, frequency_ref, start_ref,
    snd_s, rcv_s, all_s, snd_z, rcv_z, all_z, gram_s, gram_z, mine_ref, mate_ref,
    load_sem, all_s_recv, all_z_recv, gram_s_recv, gram_z_recv, mate_recv,
    freq_sem, seed_sem, sum_s_send, sum_s_recv, all_s_send,
    sum_z_send, sum_z_recv, all_z_send, gram_s_send, gram_z_send, mate_send,
):
    z = lax.axis_index("samp")
    s = lax.axis_index("snp")
    chip, core = s // 2, lax.rem(s, 2)
    chips = ns // 2
    side = math.isqrt(chips)
    halves = side // 2
    x, y = chip // side, lax.rem(chip, side)
    half = y // 2
    barrier = pltpu.get_barrier_semaphore()
    per_block = BLOCK // LANES
    owners = 2 * per_block
    every = slice(None)
    blocks_x = x_ref.shape[0] // BLOCK

    near_s = sorted(
        ((dx, dh) for dx in range(side) for dh in range(halves)), key=lambda o: (hops(o[0], side) + o[1], o)
    )
    near_z = sorted(range(nz), key=lambda o: (hops(o, nz), o))
    places = sorted(
        ((dx, dy, dc) for dx in range(side) for dy in range(side) for dc in range(2)),
        key=lambda o: (-hops(o[0], side) - hops(o[1], side), o),
    )
    places.remove((0, 0, 0))
    early_s, early_z = max(1, len(near_s) * EARLY // 8), max(1, nz * EARLY // 8)

    def block_s(offset):
        return lax.rem(x + offset[0], side) * halves + lax.rem(half + offset[1], halves)

    def chip_s(offset):
        return lax.rem(x + offset[0], side) * side + lax.rem(y + offset[1], side)

    def place_s(offset):
        return chip_s(offset) * 2 + lax.rem(core + offset[2], 2)

    def place_z(offset):
        return lax.rem(z + offset, nz)

    def span(block):
        return pl.ds(pl.multiple_of(block * BLOCK, BLOCK), BLOCK)

    def load(block):
        return pltpu.make_async_copy(geno_ref.at[span(block)], x_ref.at[span(block)], load_sem.at[block])

    load_freq = pltpu.make_async_copy(freq_ref, frequency_ref, freq_sem)
    load_seed = pltpu.make_async_copy(seed_ref, start_ref, seed_sem)
    load_freq.start()
    for offset in reversed(near_s):
        load(block_s(offset)).start()
    load_seed.start()

    @pl.loop(1, ns)
    def _(d):
        pl.semaphore_signal(barrier, 1, device_id={"snp": lax.rem(s + d, ns)}, device_id_type=MESH)

    @pl.loop(1, nz)
    def _(d):
        pl.semaphore_signal(barrier, 1, device_id={"samp": lax.rem(z + d, nz)}, device_id_type=MESH)

    def send(src, dst, send_sem, recv_sem, target):
        pltpu.make_async_remote_copy(
            src_ref=src, dst_ref=dst, send_sem=send_sem, recv_sem=recv_sem,
            device_id=target, device_id_type=MESH,
        ).start()

    def settle(ref, sem):
        pltpu.make_async_copy(ref, ref, sem).wait()

    def band_product(left):
        four = jnp.concatenate([left] * 4, axis=0)
        return lax.dot_general(left, four, (((1,), (1,)), ((), ())), preferred_element_type=jnp.float32)

    def product(ref, parts, columns):
        total = None
        for block, left in parts:
            part = jnp.dot(left, ref[span(block), columns], preferred_element_type=jnp.float32)
            total = part if total is None else total + part
        return total

    def transpose(first, last):
        @pl.loop(first, last)
        def _(i):
            @pl.loop(0, x_ref.shape[1] // BLOCK)
            def _(j):
                xt_ref[span(j), span(i)] = x_ref[span(i), span(j)].T


    others_s = pl.ds(0, ns - 1)

    def ship_s(product):
        pending = None
        for offset in reversed(near_s):
            block = block_s(offset)
            packed = product(block).astype(jnp.bfloat16)
            for t in range(owners):
                column = (t // 2) * LANES
                snd_s[block * owners + t] = packed[HALF * (t % 2) : HALF * (t % 2 + 1), column : column + LANES]
            if pending is not None:
                for t in range(owners):
                    tile = pending * owners + t
                    send(snd_s.at[tile], rcv_s.at[s], sum_s_send, sum_s_recv, {"snp": tile})
            pending = block
        for t in range(1, owners):
            tile = pending * owners + lax.rem(lax.rem(s, owners) + t, owners)
            send(snd_s.at[tile], rcv_s.at[s], sum_s_send, sum_s_recv, {"snp": tile})
        rcv_s[s] = snd_s[s]

    def finish_samples():
        settle(rcv_s.at[others_s], sum_s_recv)
        total = rcv_s[0].astype(jnp.float32)
        for i in range(1, ns):
            total = total + rcv_s[i].astype(jnp.float32)
        all_s[s] = total.astype(jnp.bfloat16)
        for offset in places:
            send(all_s.at[s], all_s.at[s], all_s_send, all_s_recv.at[chip // 2], {"snp": place_s(offset)})
        settle(snd_s.at[others_s], sum_s_send)

    def normalized(blocks, columns, out_ref):
        values = apply(factor_ref[...], jnp.concatenate(columns, axis=1))
        parts = [(block, values[:, i * BLOCK : (i + 1) * BLOCK]) for i, block in enumerate(blocks)]
        for block, part in parts:
            out_ref[:, span(block)] = part
        return parts

    def take_s(offsets):
        blocks, columns = [], []
        for offset in offsets:
            block = block_s(offset)
            settle(all_s.at[pl.ds(0, owners - (offset == (0, 0)))], all_s_recv.at[block])
            for t in range(0, owners, 2):
                columns.append(jnp.concatenate([all_s[block * owners + t], all_s[block * owners + t + 1]], axis=0))
            blocks.append(block)
        return normalized(blocks, columns, q_ref)


    others_z = pl.ds(0, nz - 1)
    other_tiles_z = pl.ds(0, (nz - 1) * per_block)

    def ship_z(product):
        pending = None

        def ship(block):
            part = pl.ds(block * per_block, per_block)
            send(snd_z.at[part], rcv_z.at[z], sum_z_send, sum_z_recv, {"samp": block})

        for offset in reversed(near_z):
            block = place_z(offset)
            packed = product(block).astype(jnp.bfloat16)
            for t in range(per_block):
                tile = packed[:, t * LANES : (t + 1) * LANES]
                if offset == 0:
                    rcv_z[z, t] = tile
                else:
                    snd_z[block * per_block + t] = tile
            if pending is not None:
                ship(pending)
            pending = block

    def finish_snps():
        settle(rcv_z.at[others_z], sum_z_recv)
        total = rcv_z[0].astype(jnp.float32)
        for i in range(1, nz):
            total = total + rcv_z[i].astype(jnp.float32)
        part = pl.ds(z * per_block, per_block)
        all_z[part] = total.astype(jnp.bfloat16)
        for offset in reversed(near_z[1:]):
            send(
                all_z.at[part], all_z.at[part], all_z_send, all_z_recv.at[nz - offset],
                {"samp": place_z(offset)},
            )
        settle(snd_z.at[other_tiles_z], sum_z_send)

    def take_z(offsets):
        blocks, columns = [], []
        for offset in offsets:
            block = place_z(offset)
            if offset != 0:
                settle(all_z.at[pl.ds(0, per_block)], all_z_recv.at[offset])
            columns += [all_z[block * per_block + t] for t in range(per_block)]
            blocks.append(block)
        return normalized(blocks, columns, p_ref)


    def send_gram_z(turn, wide):
        gram_z[turn, z] = packed_gram(wide)
        for offset in reversed(near_z[1:]):
            mine = gram_z.at[turn, z]
            send(mine, mine, gram_z_send, gram_z_recv.at[turn], {"samp": place_z(offset)})

    def take_gram_z(turn):
        settle(gram_z.at[turn, others_z], gram_z_recv.at[turn])
        settle(gram_z.at[turn, others_z], gram_z_send)
        total = gram_z[turn, 0]
        for i in range(1, nz):
            total = total + gram_z[turn, i]
        factor_ref[...] = in_parts(inverse_factor(total * (1.0 / sample_count)))

    other_chips = pl.ds(0, chips - 1)

    def send_gram_s(turn, wide):
        gram_s[turn, chip] = packed_gram(wide)
        for offset in places:
            if offset[2] == 0:
                mine = gram_s.at[turn, chip]
                send(mine, mine, gram_s_send, gram_s_recv.at[turn], {"snp": place_s(offset)})

    def take_gram_s(turn):
        settle(gram_s.at[turn, other_chips], gram_s_recv.at[turn])
        total = gram_s[turn, 0]
        for i in range(1, chips):
            total = total + gram_s[turn, i]
        mine_ref[...] = total
        send(mine_ref, mate_ref.at[turn], mate_send, mate_recv.at[turn], {"snp": s + 1 - 2 * core})
        settle(gram_s.at[turn, other_chips], gram_s_send)
        settle(mate_ref.at[turn], mate_recv.at[turn])
        settle(mine_ref, mate_send)
        total = (total + mate_ref[turn]) * (1.0 / snp_count)
        factor_ref[...] = in_parts(inverse_factor(total))

    load_freq.wait()
    double = 2.0 * frequency_ref[...]
    scale = lax.rsqrt(double * (1.0 - frequency_ref[...]))
    levels = [((dosage - double) * scale).astype(jnp.bfloat16) for dosage in (0.0, 1.0, 2.0)]
    eye = lax.broadcasted_iota(jnp.int32, (K, K), 0) == lax.broadcasted_iota(jnp.int32, (K, K), 1)
    factor_ref[...] = in_parts(jnp.where(eye, 1.0, 0.0))

    for offset in reversed(near_s):
        block = block_s(offset)
        load(block).wait()

        @pl.loop(0, BLOCK // 32)
        def _(i):
            lines = pl.ds(pl.multiple_of(block * BLOCK + i * 32, 32), 32)
            values = x_ref[lines, :]
            known = jnp.where(
                values == 0.0, levels[0], jnp.where(values == 1.0, levels[1], levels[2])
            )
            x_ref[lines, :] = jnp.where(values < 3.0, known, jnp.bfloat16(0.0))

    load_seed.wait()
    seed = start_ref[...].astype(jnp.bfloat16)
    pl.semaphore_wait(barrier, ns - 1 + nz - 1)
    ship_s(
        lambda block: lax.dot_general(
            seed, x_ref[span(block), :], (((1,), (1,)), ((), ())), preferred_element_type=jnp.float32
        )
    )
    transpose(0, blocks_x // 2)
    finish_samples()
    transpose(blocks_x // 2, blocks_x)

    def to_snps(turn):
        acc_ref[...] = product(x_ref, take_s(near_s[:early_s]), every)
        late = take_s(near_s[early_s:])
        ship_z(lambda out: acc_ref[:, span(out)] + product(x_ref, late, span(out)))
        send_gram_z(turn, band_product(q_ref[...]))
        settle(rcv_s.at[others_s], all_s_send)
        finish_snps()
        take_gram_z(turn)

    def to_samples(turn):
        acc_ref[...] = product(xt_ref, take_z(near_z[:early_z]), every)
        late = take_z(near_z[early_z:])
        ship_s(lambda out: acc_ref[:, span(out)] + product(xt_ref, late, span(out)))
        send_gram_s(turn, band_product(p_ref[...]))
        settle(all_z.at[other_tiles_z], all_z_send)
        finish_samples()
        take_gram_s(turn)

    @pl.loop(0, ITERS)
    def _(i):
        turn = lax.rem(i, 2)
        to_snps(turn)
        to_samples(turn)

    final = ITERS % 2
    for block in range(p_ref.shape[1] // BLOCK):
        columns = slice(block * BLOCK, (block + 1) * BLOCK)
        p_ref[:, columns] = apply(factor_ref[...], p_ref[:, columns])
    take_s(near_s)
    send_gram_z(final, band_product(q_ref[...]))
    settle(rcv_s.at[others_s], all_s_send)
    take_gram_z(final)
    for block in range(q_ref.shape[1] // BLOCK):
        columns = slice(block * BLOCK, (block + 1) * BLOCK)
        q_ref[:, columns] = apply(factor_ref[...], q_ref[:, columns])


def per_device(nz, ns, genotypes, frequency, seed_matrix):
    samples, snps = genotypes.shape
    tiles_s, tiles_z, chips = samples // LANES, snps // LANES, ns // 2
    bf16, f32 = jnp.bfloat16, jnp.float32
    vmem, hbm = pl.BlockSpec(memory_space=pltpu.VMEM), pl.BlockSpec(memory_space=pl.ANY)
    dma = pltpu.SemaphoreType.DMA
    return pl.pallas_call(
        functools.partial(kernel, nz, ns, float(samples * nz), float(snps * ns)),
        out_shape=(
            jax.ShapeDtypeStruct((K, samples), bf16),
            jax.ShapeDtypeStruct((K, snps), bf16),
        ),
        in_specs=[hbm, hbm, hbm],
        out_specs=(vmem, vmem),
        scratch_shapes=[
            pltpu.VMEM((samples, snps), bf16),
            pltpu.VMEM((snps, samples), bf16),
            pltpu.VMEM((K, max(samples, snps)), f32),
            pltpu.VMEM((3 * K, K), bf16),
            pltpu.VMEM((1, snps), f32),
            pltpu.VMEM((K, snps), f32),
            pltpu.VMEM((ns, HALF, LANES), bf16),
            pltpu.VMEM((ns, HALF, LANES), bf16),
            pltpu.VMEM((ns, HALF, LANES), bf16),
            pltpu.VMEM((tiles_z, K, LANES), bf16),
            pltpu.VMEM((nz, tiles_z // nz, K, LANES), bf16),
            pltpu.VMEM((tiles_z, K, LANES), bf16),
            pltpu.VMEM((2, chips, 8, LANES), f32),
            pltpu.VMEM((2, nz, 8, LANES), f32),
            pltpu.VMEM((8, LANES), f32),
            pltpu.VMEM((2, 8, LANES), f32),
            dma((samples // BLOCK,)),
            dma((samples // BLOCK,)),
            dma((nz,)),
            dma((2,)),
            dma((2,)),
            dma((2,)),
        ]
        + [dma(())] * 11,
        compiler_params=pltpu.CompilerParams(
            collective_id=0, has_side_effects=True, vmem_limit_bytes=48 * 1024 * 1024
        ),
    )(genotypes, frequency.reshape(1, snps), seed_matrix)


def solution(mesh):
    placed = (P("samp", "snp"), P("snp"), P(None, "snp"))
    return jax.shard_map(
        functools.partial(per_device, mesh.shape["samp"], mesh.shape["snp"]),
        mesh=mesh,
        in_specs=placed,
        out_specs=(P(None, "samp"), P(None, "snp")),
        check_vma=False,
    )
```

```python
import functools
import math

import jax
import jax.numpy as jnp
from jax import lax
from jax.experimental import pallas as pl
from jax.experimental.pallas import tpu as pltpu
from jax.sharding import PartitionSpec as P

ITERS = 6
K = 32
LANES = 128
BLOCK = 256
PANEL = 8
GROUPS_S = (4, 3, 1)
GROUPS_Z = (3, 2, 3)
MESH = pl.DeviceIdType.MESH
HALF = K // 2


def hops(offset, count):
    return min(offset, count - offset)


def in_parts(factor):
    high = factor.astype(jnp.bfloat16)
    rest = factor - high.astype(jnp.float32)
    middle = rest.astype(jnp.bfloat16)
    low = (rest - middle.astype(jnp.float32)).astype(jnp.bfloat16)
    return jnp.concatenate([high, middle, low], axis=0)


def apply(parts, values):
    three = jnp.dot(parts, values, preferred_element_type=jnp.float32)
    return (three[:K] + three[K : 2 * K] + three[2 * K :]).astype(jnp.bfloat16)


def packed_gram(wide):
    band = lax.broadcasted_iota(jnp.int32, (8, LANES), 1) // K
    out = wide[0:8]
    for b in range(1, 4):
        out = jnp.where(band == b, wide[8 * b : 8 * b + 8], out)
    return out


def inverse_factor(packed):
    lane = lax.broadcasted_iota(jnp.int32, (8, LANES), 1)
    row = lax.broadcasted_iota(jnp.int32, (8, LANES), 0)
    bands = []
    for b in range(4):
        shift = (K - K * b) % LANES
        band = pltpu.roll(packed, shift, 1) if shift else packed
        bands.append(jnp.where(lane < K, jnp.where(lane == row + 8 * b, 1.0, 0.0), band))
    for p in range(K // PANEL):
        start = K + PANEL * p
        columns = [
            [jnp.broadcast_to(bands[b][:, start + c : start + c + 1], (8, LANES)) for b in range(p, 4)]
            for c in range(PANEL)
        ]
        for c in range(PANEL):
            inverse = 1.0 / columns[c][0][c : c + 1, :]
            line = bands[p][c : c + 1, :] * inverse
            heads = [columns[d][0][c : c + 1, :] * inverse for d in range(c + 1, PANEL)]
            for b in range(p, 4):
                share = columns[c][b - p]
                if b == p:
                    share = jnp.where(row > c, share, 0.0)
                bands[b] = bands[b] - share * line
                for d in range(c + 1, PANEL):
                    columns[d][b - p] = columns[d][b - p] - share * heads[d - c - 1]
    out = []
    for b in range(4):
        diagonal = jnp.sum(jnp.where(lane == row + K + 8 * b, bands[b], 0.0), axis=1, keepdims=True)
        out.append(bands[b] * lax.rsqrt(diagonal))
    return jnp.concatenate(out, axis=0)[:, :K]


def kernel(
    nz, ns, sample_count, snp_count,
    geno_ref, freq_ref, seed_ref, q_ref, p_ref,
    x_ref, xt_ref, acc_ref, factor_ref, frequency_ref, start_ref,
    snd_s, rcv_s, all_s, snd_z, rcv_z, all_z, gram_s, gram_z, mine_ref, mate_ref,
    load_sem, all_s_recv, all_z_recv, gram_s_recv, gram_z_recv, mate_recv,
    freq_sem, seed_sem, sum_s_send, sum_s_recv, all_s_send,
    sum_z_send, sum_z_recv, all_z_send, gram_s_send, gram_z_send, mate_send,
):
    z = lax.axis_index("samp")
    s = lax.axis_index("snp")
    chip, core = s // 2, lax.rem(s, 2)
    chips = ns // 2
    side = math.isqrt(chips)
    halves = side // 2
    x, y = chip // side, lax.rem(chip, side)
    half = y // 2
    barrier = pltpu.get_barrier_semaphore()
    per_block = BLOCK // LANES
    owners = 2 * per_block
    every = slice(None)
    blocks_x = x_ref.shape[0] // BLOCK

    near_s = sorted(
        ((dx, dh) for dx in range(side) for dh in range(halves)), key=lambda o: (hops(o[0], side) + o[1], o)
    )
    near_z = sorted(range(nz), key=lambda o: (hops(o, nz), o))
    places = sorted(
        ((dx, dy, dc) for dx in range(side) for dy in range(side) for dc in range(2)),
        key=lambda o: (-hops(o[0], side) - hops(o[1], side), o),
    )
    places.remove((0, 0, 0))

    def block_s(offset):
        return lax.rem(x + offset[0], side) * halves + lax.rem(half + offset[1], halves)

    def chip_s(offset):
        return lax.rem(x + offset[0], side) * side + lax.rem(y + offset[1], side)

    def place_s(offset):
        return chip_s(offset) * 2 + lax.rem(core + offset[2], 2)

    def place_z(offset):
        return lax.rem(z + offset, nz)

    def span(block):
        return pl.ds(pl.multiple_of(block * BLOCK, BLOCK), BLOCK)

    def load(block):
        return pltpu.make_async_copy(geno_ref.at[span(block)], x_ref.at[span(block)], load_sem.at[block])

    load_freq = pltpu.make_async_copy(freq_ref, frequency_ref, freq_sem)
    load_seed = pltpu.make_async_copy(seed_ref, start_ref, seed_sem)
    load_freq.start()
    load_seed.start()
    for offset in reversed(near_s):
        load(block_s(offset)).start()

    @pl.loop(1, ns)
    def _(d):
        pl.semaphore_signal(barrier, 1, device_id={"snp": lax.rem(s + d, ns)}, device_id_type=MESH)

    @pl.loop(1, nz)
    def _(d):
        pl.semaphore_signal(barrier, 1, device_id={"samp": lax.rem(z + d, nz)}, device_id_type=MESH)

    def send(src, dst, send_sem, recv_sem, target):
        pltpu.make_async_remote_copy(
            src_ref=src, dst_ref=dst, send_sem=send_sem, recv_sem=recv_sem,
            device_id=target, device_id_type=MESH,
        ).start()

    def settle(ref, sem):
        pltpu.make_async_copy(ref, ref, sem).wait()

    def band_product(left):
        four = jnp.concatenate([left] * 4, axis=0)
        return lax.dot_general(left, four, (((1,), (1,)), ((), ())), preferred_element_type=jnp.float32)

    def product(ref, parts, columns):
        total = None
        for block, left in parts:
            part = jnp.dot(left, ref[span(block), columns], preferred_element_type=jnp.float32)
            total = part if total is None else total + part
        return total

    def early_products(ref, take, near, sizes):
        groups, start = [], 0
        for size in sizes:
            groups.append(near[start : start + size])
            start += size
        groups = [group for group in groups[:-1] if group] + [near[start - sizes[-1] :]]
        if len(near) < start:
            groups = [near[:1], near[1:]]
        for i, group in enumerate(groups[:-1]):
            values = product(ref, take(group), every)
            acc_ref[...] = values if i == 0 else acc_ref[...] + values
        return take(groups[-1])

    def transpose(first, last):
        @pl.loop(first, last)
        def _(i):
            @pl.loop(0, x_ref.shape[1] // BLOCK)
            def _(j):
                xt_ref[span(j), span(i)] = x_ref[span(i), span(j)].T


    others_s = pl.ds(0, ns - 1)

    def ship_s(product):
        pending = None
        for offset in reversed(near_s):
            block = block_s(offset)
            packed = product(block).astype(jnp.bfloat16)
            for t in range(owners):
                column = (t // 2) * LANES
                snd_s[block * owners + t] = packed[HALF * (t % 2) : HALF * (t % 2 + 1), column : column + LANES]
            if pending is not None:
                for t in range(owners):
                    tile = pending * owners + t
                    send(snd_s.at[tile], rcv_s.at[s], sum_s_send, sum_s_recv, {"snp": tile})
            pending = block
        for t in range(1, owners):
            tile = pending * owners + lax.rem(lax.rem(s, owners) + t, owners)
            send(snd_s.at[tile], rcv_s.at[s], sum_s_send, sum_s_recv, {"snp": tile})
        rcv_s[s] = snd_s[s]

    def finish_samples():
        settle(rcv_s.at[others_s], sum_s_recv)
        total = rcv_s[0].astype(jnp.float32)
        for i in range(1, ns):
            total = total + rcv_s[i].astype(jnp.float32)
        all_s[s] = total.astype(jnp.bfloat16)
        for offset in places:
            send(all_s.at[s], all_s.at[s], all_s_send, all_s_recv.at[chip // 2], {"snp": place_s(offset)})
        settle(snd_s.at[others_s], sum_s_send)

    def normalized(blocks, columns, out_ref):
        values = apply(factor_ref[...], jnp.concatenate(columns, axis=1))
        parts = [(block, values[:, i * BLOCK : (i + 1) * BLOCK]) for i, block in enumerate(blocks)]
        for block, part in parts:
            out_ref[:, span(block)] = part
        return parts

    def take_s(offsets):
        blocks, columns = [], []
        for offset in offsets:
            block = block_s(offset)
            settle(all_s.at[pl.ds(0, owners - (offset == (0, 0)))], all_s_recv.at[block])
            for t in range(0, owners, 2):
                columns.append(jnp.concatenate([all_s[block * owners + t], all_s[block * owners + t + 1]], axis=0))
            blocks.append(block)
        return normalized(blocks, columns, q_ref)


    others_z = pl.ds(0, nz - 1)
    other_tiles_z = pl.ds(0, (nz - 1) * per_block)

    def ship_z(product):
        pending = None

        def ship(block):
            part = pl.ds(block * per_block, per_block)
            send(snd_z.at[part], rcv_z.at[z], sum_z_send, sum_z_recv, {"samp": block})

        for offset in reversed(near_z):
            block = place_z(offset)
            packed = product(block).astype(jnp.bfloat16)
            for t in range(per_block):
                tile = packed[:, t * LANES : (t + 1) * LANES]
                if offset == 0:
                    rcv_z[z, t] = tile
                else:
                    snd_z[block * per_block + t] = tile
            if pending is not None:
                ship(pending)
            pending = block

    def finish_snps():
        settle(rcv_z.at[others_z], sum_z_recv)
        total = rcv_z[0].astype(jnp.float32)
        for i in range(1, nz):
            total = total + rcv_z[i].astype(jnp.float32)
        part = pl.ds(z * per_block, per_block)
        all_z[part] = total.astype(jnp.bfloat16)
        for offset in reversed(near_z[1:]):
            send(
                all_z.at[part], all_z.at[part], all_z_send, all_z_recv.at[nz - offset],
                {"samp": place_z(offset)},
            )
        settle(snd_z.at[other_tiles_z], sum_z_send)

    def take_z(offsets):
        blocks, columns = [], []
        for offset in offsets:
            block = place_z(offset)
            if offset != 0:
                settle(all_z.at[pl.ds(0, per_block)], all_z_recv.at[offset])
            columns += [all_z[block * per_block + t] for t in range(per_block)]
            blocks.append(block)
        return normalized(blocks, columns, p_ref)


    def send_gram_z(turn, wide):
        gram_z[turn, z] = packed_gram(wide)
        for offset in reversed(near_z[1:]):
            mine = gram_z.at[turn, z]
            send(mine, mine, gram_z_send, gram_z_recv.at[turn], {"samp": place_z(offset)})

    def take_gram_z(turn):
        settle(gram_z.at[turn, others_z], gram_z_recv.at[turn])
        settle(gram_z.at[turn, others_z], gram_z_send)
        total = gram_z[turn, 0]
        for i in range(1, nz):
            total = total + gram_z[turn, i]
        factor_ref[...] = in_parts(inverse_factor(total * (1.0 / sample_count)))

    other_chips = pl.ds(0, chips - 1)

    def send_gram_s(turn, wide):
        gram_s[turn, chip] = packed_gram(wide)
        for offset in places:
            if offset[2] == 0:
                mine = gram_s.at[turn, chip]
                send(mine, mine, gram_s_send, gram_s_recv.at[turn], {"snp": place_s(offset)})

    def take_gram_s(turn):
        settle(gram_s.at[turn, other_chips], gram_s_recv.at[turn])
        total = gram_s[turn, 0]
        for i in range(1, chips):
            total = total + gram_s[turn, i]
        mine_ref[...] = total
        send(mine_ref, mate_ref.at[turn], mate_send, mate_recv.at[turn], {"snp": s + 1 - 2 * core})
        settle(gram_s.at[turn, other_chips], gram_s_send)
        settle(mate_ref.at[turn], mate_recv.at[turn])
        settle(mine_ref, mate_send)
        total = (total + mate_ref[turn]) * (1.0 / snp_count)
        factor_ref[...] = in_parts(inverse_factor(total))

    load_freq.wait()
    double = 2.0 * frequency_ref[...]
    scale = lax.rsqrt(double * (1.0 - frequency_ref[...]))
    levels = [((dosage - double) * scale).astype(jnp.bfloat16) for dosage in (0.0, 1.0, 2.0)]
    eye = lax.broadcasted_iota(jnp.int32, (K, K), 0) == lax.broadcasted_iota(jnp.int32, (K, K), 1)
    factor_ref[...] = in_parts(jnp.where(eye, 1.0, 0.0))

    load_seed.wait()
    seed = start_ref[...].astype(jnp.bfloat16)
    pl.semaphore_wait(barrier, ns - 1 + nz - 1)

    def first_product(block):
        load(block).wait()

        @pl.loop(0, BLOCK // 32)
        def _(i):
            lines = pl.ds(pl.multiple_of(block * BLOCK + i * 32, 32), 32)
            values = x_ref[lines, :]
            known = jnp.where(
                values == 0.0, levels[0], jnp.where(values == 1.0, levels[1], levels[2])
            )
            x_ref[lines, :] = jnp.where(values < 3.0, known, jnp.bfloat16(0.0))

        return lax.dot_general(
            seed, x_ref[span(block), :], (((1,), (1,)), ((), ())), preferred_element_type=jnp.float32
        )

    ship_s(first_product)
    transpose(0, blocks_x // 2)
    finish_samples()
    transpose(blocks_x // 2, blocks_x)

    def to_snps(turn):
        late = early_products(x_ref, take_s, near_s, GROUPS_S)
        ship_z(lambda out: acc_ref[:, span(out)] + product(x_ref, late, span(out)))
        send_gram_z(turn, band_product(q_ref[...]))
        settle(rcv_s.at[others_s], all_s_send)
        finish_snps()
        take_gram_z(turn)

    def to_samples(turn):
        late = early_products(xt_ref, take_z, near_z, GROUPS_Z)
        ship_s(lambda out: acc_ref[:, span(out)] + product(xt_ref, late, span(out)))
        send_gram_s(turn, band_product(p_ref[...]))
        settle(all_z.at[other_tiles_z], all_z_send)
        finish_samples()
        take_gram_s(turn)

    @pl.loop(0, ITERS)
    def _(i):
        turn = lax.rem(i, 2)
        to_snps(turn)
        to_samples(turn)

    final = ITERS % 2
    for block in range(p_ref.shape[1] // BLOCK):
        columns = slice(block * BLOCK, (block + 1) * BLOCK)
        p_ref[:, columns] = apply(factor_ref[...], p_ref[:, columns])
    take_s(near_s)
    send_gram_z(final, band_product(q_ref[...]))
    settle(rcv_s.at[others_s], all_s_send)
    take_gram_z(final)
    for block in range(q_ref.shape[1] // BLOCK):
        columns = slice(block * BLOCK, (block + 1) * BLOCK)
        q_ref[:, columns] = apply(factor_ref[...], q_ref[:, columns])


def per_device(nz, ns, genotypes, frequency, seed_matrix):
    samples, snps = genotypes.shape
    tiles_s, tiles_z, chips = samples // LANES, snps // LANES, ns // 2
    bf16, f32 = jnp.bfloat16, jnp.float32
    vmem, hbm = pl.BlockSpec(memory_space=pltpu.VMEM), pl.BlockSpec(memory_space=pl.ANY)
    dma = pltpu.SemaphoreType.DMA
    return pl.pallas_call(
        functools.partial(kernel, nz, ns, float(samples * nz), float(snps * ns)),
        out_shape=(
            jax.ShapeDtypeStruct((K, samples), bf16),
            jax.ShapeDtypeStruct((K, snps), bf16),
        ),
        in_specs=[hbm, hbm, hbm],
        out_specs=(vmem, vmem),
        scratch_shapes=[
            pltpu.VMEM((samples, snps), bf16),
            pltpu.VMEM((snps, samples), bf16),
            pltpu.VMEM((K, max(samples, snps)), f32),
            pltpu.VMEM((3 * K, K), bf16),
            pltpu.VMEM((1, snps), f32),
            pltpu.VMEM((K, snps), f32),
            pltpu.VMEM((ns, HALF, LANES), bf16),
            pltpu.VMEM((ns, HALF, LANES), bf16),
            pltpu.VMEM((ns, HALF, LANES), bf16),
            pltpu.VMEM((tiles_z, K, LANES), bf16),
            pltpu.VMEM((nz, tiles_z // nz, K, LANES), bf16),
            pltpu.VMEM((tiles_z, K, LANES), bf16),
            pltpu.VMEM((2, chips, 8, LANES), f32),
            pltpu.VMEM((2, nz, 8, LANES), f32),
            pltpu.VMEM((8, LANES), f32),
            pltpu.VMEM((2, 8, LANES), f32),
            dma((samples // BLOCK,)),
            dma((samples // BLOCK,)),
            dma((nz,)),
            dma((2,)),
            dma((2,)),
            dma((2,)),
        ]
        + [dma(())] * 11,
        compiler_params=pltpu.CompilerParams(
            collective_id=0, has_side_effects=True, vmem_limit_bytes=48 * 1024 * 1024
        ),
    )(genotypes, frequency.reshape(1, snps), seed_matrix)


def solution(mesh):
    placed = (P("samp", "snp"), P("snp"), P(None, "snp"))
    return jax.shard_map(
        functools.partial(per_device, mesh.shape["samp"], mesh.shape["snp"]),
        mesh=mesh,
        in_specs=placed,
        out_specs=(P(None, "samp"), P(None, "snp")),
        check_vma=False,
    )
```
